32 devices in a mesh: groups: 2 (over x), tm: 16 (over z, y, core).
Axes of the slice: x: 2, y: 2, z: 4, core: 2. Of those that a mesh axis runs over, the one named last changes fastest.
Arguments:
- features: bfloat16 [32, 256, 384], P(('groups', 'tm')), parts along dimension 0, may hold values from -22 to 22
- lists: int32 [4, 32, 2, 2], P(None, ('groups', 'tm')), parts along dimension 1, may hold values from 0 to 1, as said below
- w_qk: bfloat16 [384, 384], replicated, may hold values from -0.3125 to 0.3125
- w_v: bfloat16 [384, 384], replicated, may hold values from -0.3125 to 0.3125
- w_out: bfloat16 [384, 384], replicated, may hold values from -0.3125 to 0.3125
- cotangent: bfloat16 [32, 256, 384], P(('groups', 'tm')), parts along dimension 0, may hold values from -6 to 6
Outputs:
- grad_features: bfloat16 [32, 256, 384], P(('groups', 'tm')), parts along dimension 0
- grad_qk: float32 [768, 384], P('groups'), parts along dimension 0
- grad_v: float32 [768, 384], P('groups'), parts along dimension 0
- grad_out: float32 [768, 384], P('groups'), parts along dimension 0
The draws below stay inside these ranges and needn't reach their ends.
There are 2 independent parts, one for each index of `groups`. The reference program is written for one: setup_inputs(seed, part) draws one part's arguments, and reference() takes and returns one part's arrays. A program takes and returns all parts, laid end to end along the dimension named above; an argument that names none is the same for every part. Nothing has to cross between parts.
Inputs may be any that keep to these rules, and one draw needn't show every extreme that they name: `lists`: entry 0 of every list is the query block's own index; the 2 entries of a list differ.
All inputs are finite; a program needn't handle non-finite values.
Results may differ from the reference program's by a relative error of at most 0.015.
The reference program's roundings to bfloat16 on the way count: a program that leaves them out, or rounds other values in their place, can miss the bound.
Values may be sent and summed in bfloat16 or wider, within the bound.
A program may use at most 64 MiB of HBM per device.

```python
import math
import jax
import jax.numpy as jnp
from jax import lax

D = 384
HEADS = 6
TOK = 256
BLK = 128
KB = 2
NG = 4
FRAMES = 16
TOKENS = 4096


def draw_features(key, part):
    base = jax.random.truncated_normal(jax.random.fold_in(key, 11), -4.0, 4.0, (FRAMES, TOK, D), jnp.float32)
    return base.astype(jnp.bfloat16)


def draw_lists(key, part):
    block_ids = jnp.broadcast_to(jnp.arange(TOK // BLK, dtype=jnp.int32)[None, None, :, None], (NG, FRAMES, TOK // BLK, 1))
    offsets = jax.random.randint(jax.random.fold_in(key, 21), (NG, FRAMES, TOK // BLK, KB - 1), 1, TOK // BLK)
    others = (block_ids + offsets) % (TOK // BLK)
    return jnp.concatenate([block_ids, others], axis=-1).astype(jnp.int32)


def level_of(rng, dims, cuts, low, largest):
    gain, own = 1.0, jax.random.fold_in(rng, 6)
    for axis_at, blocks in cuts:
        steps = jnp.exp(jax.random.uniform(jax.random.fold_in(own, axis_at), (blocks,), jnp.float32, low / len(cuts), largest / len(cuts)))
        gain = gain * jnp.repeat(steps, dims[axis_at] // blocks).reshape([-1 if axis == axis_at else 1 for axis in range(len(dims))])
    return gain


def normal_values(key, dims, width, limit, cuts=(), held_as=jnp.bfloat16):
    entries = jax.random.normal(key, dims, jnp.float32) * width
    if len(cuts) > 0:
        entries = level_of(key, dims, cuts, -0.22, 0.18) * entries
    return jnp.clip(entries, min=-limit, max=limit).astype(held_as)


def setup_inputs(seed: int = 0, part: int = 0) -> dict:
    splits = jax.random.split(jax.random.key(seed), 7)
    part_splits = jax.random.split(jax.random.fold_in(splits[6], part), 7)
    features = draw_features(jax.random.fold_in(jax.random.fold_in(splits[6], part), 71), part)
    lists = draw_lists(jax.random.fold_in(jax.random.fold_in(splits[6], part), 71), part)
    w_qk = normal_values(splits[2], (D, D), D ** -0.5, 0.3125)
    w_v = normal_values(splits[3], (D, D), D ** -0.5, 0.3125)
    w_out = normal_values(splits[4], (D, D), D ** -0.5, 0.3125)
    cotangent = normal_values(part_splits[5], (FRAMES, TOK, D), 1.0, 6.0, ((0, 16),))
    return {"features": features, "lists": lists, "w_qk": w_qk, "w_v": w_v, "w_out": w_out, "cotangent": cotangent}


def take_blocks(source, block_list):
    block_count = block_list.shape[0]
    blocks = source.reshape(block_count, -1, source.shape[-1])
    picked = jnp.take(blocks, block_list, axis=0)
    return picked.reshape(block_count, -1, HEADS, source.shape[-1] // HEADS)

def probabilities(queries, key_rows, block_list):
    block_count = block_list.shape[0]
    head_size = queries.shape[-1] // HEADS
    q_heads = queries.reshape(block_count, -1, HEADS, head_size)
    k_heads = take_blocks(key_rows, block_list)
    scores = jnp.einsum('nqhd,nkhd->nhqk', q_heads.astype(jnp.float32), k_heads.astype(jnp.float32)) * (1.0 / math.sqrt(head_size))
    return (q_heads, k_heads, jax.nn.softmax(scores, axis=-1))

def add_blocks(block_terms, block_list, out_shape):
    block_count, list_length = block_list.shape
    pieces = block_terms.reshape(block_count, list_length, -1, out_shape[-1])
    summed = jnp.zeros((block_count, pieces.shape[2], out_shape[-1]), jnp.float32).at[block_list].add(pieces)
    return summed.reshape(out_shape)

def attend_forward(queries, key_rows, value_rows, block_list):
    q_heads, k_heads, probs_full = probabilities(queries, key_rows, block_list)
    v_heads = take_blocks(value_rows, block_list)
    weights = probs_full.astype(jnp.bfloat16)
    mixed_out = jnp.einsum('nhqk,nkhd->nqhd', weights.astype(jnp.float32), v_heads.astype(jnp.float32))
    return mixed_out.reshape(queries.shape).astype(jnp.bfloat16)

def attend_backward(queries, key_rows, value_rows, block_list, upstream, result):
    q_heads, k_heads, probs_full = probabilities(queries, key_rows, block_list)
    v_heads = take_blocks(value_rows, block_list)
    weights = probs_full.astype(jnp.bfloat16)
    inv_root = 1.0 / math.sqrt(queries.shape[-1] // HEADS)
    up_heads = upstream.reshape(q_heads.shape)
    res_heads = result.reshape(q_heads.shape)
    d_probs = jnp.einsum('nqhd,nkhd->nhqk', up_heads.astype(jnp.float32), v_heads.astype(jnp.float32))
    row_sums = jnp.swapaxes(lax.optimization_barrier(jnp.sum(up_heads.astype(jnp.float32) * res_heads.astype(jnp.float32), axis=-1)), 1, 2)
    d_scores = probs_full * (d_probs - row_sums[..., None])
    d_rounded = d_scores.astype(jnp.bfloat16)
    d_query = jnp.einsum('nhqk,nkhd->nqhd', d_rounded.astype(jnp.float32), k_heads.astype(jnp.float32)) * inv_root
    d_keys = jnp.einsum('nhqk,nqhd->nkhd', d_rounded.astype(jnp.float32), q_heads.astype(jnp.float32)) * inv_root
    d_values = jnp.einsum('nhqk,nqhd->nkhd', weights.astype(jnp.float32), up_heads.astype(jnp.float32))
    key_grad = add_blocks(d_keys, block_list, queries.shape).astype(jnp.bfloat16)
    value_grad = add_blocks(d_values, block_list, queries.shape).astype(jnp.bfloat16)
    return (d_query.reshape(queries.shape), key_grad, value_grad)

def partner_of(source, gap_size):
    filler = jnp.zeros((gap_size,) + source.shape[1:], source.dtype)
    return jnp.concatenate([source[gap_size:], filler], axis=0)

def reference(features, lists, w_qk, w_v, w_out, cotangent):
    flat = features.reshape(-1, D)
    shared = jnp.dot(flat, w_qk, preferred_element_type=jnp.float32).astype(jnp.bfloat16).reshape(FRAMES, TOK, D)
    values = jnp.dot(flat, w_v, preferred_element_type=jnp.float32).astype(jnp.bfloat16).reshape(FRAMES, TOK, D)
    frame_ids = jnp.arange(FRAMES)
    outputs = []
    for gap_index in range(NG):
        gap_size = 2 ** gap_index
        valid = (frame_ids + gap_size < FRAMES)[:, None, None]
        mixed_out = lax.map(lambda packed: attend_forward(*packed), (shared, partner_of(shared, gap_size), partner_of(values, gap_size), lists[gap_index]))
        outputs.append(jnp.where(valid, mixed_out, jnp.zeros_like(mixed_out)))
    summed = jnp.zeros((FRAMES, TOK, D), jnp.float32)
    for mixed_out in outputs:
        summed = summed + mixed_out.astype(jnp.float32)
    hidden = summed.astype(jnp.bfloat16).reshape(-1, D)
    grad_flat = cotangent.reshape(-1, D)
    out_part = jnp.dot(hidden.T, grad_flat, preferred_element_type=jnp.float32)
    d_hidden = jnp.dot(grad_flat, w_out.T, preferred_element_type=jnp.float32).astype(jnp.bfloat16).reshape(FRAMES, TOK, D)
    query_sum = jnp.zeros((FRAMES, TOK, D), jnp.float32)
    key_sum = jnp.zeros((FRAMES, TOK, D), jnp.float32)
    wqk_part = jnp.zeros((D, D), jnp.float32)
    wv_part = jnp.zeros((D, D), jnp.float32)
    for gap_index in range(NG):
        gap_size = 2 ** gap_index
        valid = (frame_ids + gap_size < FRAMES)[:, None, None]
        d_query, key_grad, value_grad = lax.map(lambda packed: attend_backward(*packed), (shared, partner_of(shared, gap_size), partner_of(values, gap_size), lists[gap_index], d_hidden, outputs[gap_index]))
        d_query = jnp.where(valid, d_query, jnp.zeros_like(d_query))
        key_grad = jnp.where(valid, key_grad, jnp.zeros_like(key_grad))
        value_grad = jnp.where(valid, value_grad, jnp.zeros_like(value_grad))
        query_sum = query_sum + d_query
        key_flat = key_grad.reshape(-1, D)
        value_flat = value_grad.reshape(-1, D)
        partner_rows = partner_of(features, gap_size).reshape(-1, D)
        wqk_part = wqk_part + jnp.dot(partner_rows.T, key_flat, preferred_element_type=jnp.float32)
        wv_part = wv_part + jnp.dot(partner_rows.T, value_flat, preferred_element_type=jnp.float32)
        key_term = (jnp.dot(key_flat, w_qk.T, preferred_element_type=jnp.float32) + jnp.dot(value_flat, w_v.T, preferred_element_type=jnp.float32)).astype(jnp.bfloat16)
        key_term = lax.optimization_barrier(key_term).astype(jnp.float32).reshape(FRAMES, TOK, D)
        moved = jnp.concatenate([jnp.zeros((gap_size, TOK, D), jnp.float32), key_term[:FRAMES - gap_size]], axis=0)
        key_sum = key_sum + moved
    query_grad = query_sum.astype(jnp.bfloat16).reshape(-1, D)
    wqk_part = wqk_part + jnp.dot(flat.T, query_grad, preferred_element_type=jnp.float32)
    grad_features = (jnp.dot(query_grad, w_qk.T, preferred_element_type=jnp.float32).reshape(FRAMES, TOK, D) + key_sum).astype(jnp.bfloat16)
    norm_factor = 1.0 / math.sqrt(TOKENS)
    return (grad_features, wqk_part * norm_factor, wv_part * norm_factor, out_part * norm_factor)
```

```python
import functools
import math

import jax
import jax.numpy as jnp
from jax import lax
from jax.experimental import pallas as pl
from jax.experimental.pallas import tpu as pltpu
from jax.sharding import PartitionSpec as P

HEADS = 6
NG = 4
ORDER = (1, 0, 3, 2)
MESH = pl.DeviceIdType.MESH
F32 = jnp.float32
BF16 = jnp.bfloat16


def dot(left, right, dims=((1,), (0,))):
    return lax.dot_general(left, right, (dims, ((), ())), preferred_element_type=F32)


def bits_of(count):
    return [2**i for i in range(count.bit_length() - 1)]


def halving_steps(rows, count):
    steps = 0
    while steps < len(bits_of(count)) - 1 and rows % 32 == 0:
        rows //= 2
        steps += 1
    return steps


def kernel(
    count, x_hbm, cot_hbm, wqk_hbm, wv_hbm, wout_hbm, grad_hbm, weights_hbm,
    x_ref, cot_ref, wqk_ref, wv_ref, wout_ref, in_sem, grad_out, wcat, wcat_t, q_t, dh_t, kv_t, dkv_t, dq_t, hid_t,
    partner, kt_send, kt_recv, acc, outgoing, result, *rest,
):
    width = wqk_ref.shape[0]
    head = width // HEADS
    bits = bits_of(count)
    halvings = halving_steps(width, count)
    landing = rest[: len(bits)]
    again = rest[len(bits)]
    f_send, f_recv, k_send, k_recv, a_send, a_recv = rest[len(bits) + 1 :]
    me = lax.axis_index("tm")
    gaps = [2**j for j in range(NG)]

    loads = [
        pltpu.make_async_copy(source, target, in_sem.at[i])
        for i, (source, target) in enumerate((
            (x_hbm, x_ref), (wqk_hbm, wqk_ref), (wv_hbm, wv_ref), (cot_hbm, cot_ref),
            (wout_hbm, wout_ref),
        ))
    ]
    for load in loads:
        load.start()

    barrier = pltpu.get_barrier_semaphore()
    expected = jnp.int32(0)
    for gap in gaps:
        for valid, other in ((me >= gap, me - gap), (me + gap < count, me + gap)):
            @pl.when(valid)
            def _(other=other):
                pl.semaphore_signal(barrier, inc=1, device_id={"tm": other}, device_id_type=MESH)
            expected = expected + jnp.where(valid, 1, 0)
    flips = [me + bit * (1 - 2 * ((me // bit) % 2)) for bit in bits]
    for bit, other in zip(bits, flips):
        if bit not in gaps:
            pl.semaphore_signal(barrier, inc=1, device_id={"tm": other}, device_id_type=MESH)
            expected = expected + 1
    pl.semaphore_wait(barrier, expected)

    def feature_copy(j, other, source=x_hbm):
        return pltpu.make_async_remote_copy(
            src_ref=source, dst_ref=partner.at[j], send_sem=f_send.at[j], recv_sem=f_recv.at[j],
            device_id={"tm": other}, device_id_type=MESH,
        )

    def term_copy(j, other):
        return pltpu.make_async_remote_copy(
            src_ref=kt_send.at[j], dst_ref=kt_recv.at[j], send_sem=k_send.at[j],
            recv_sem=k_recv.at[j], device_id={"tm": other}, device_id_type=MESH,
        )

    odd = me % 2 == 1
    passes_one = jnp.logical_and(jnp.logical_not(odd), me + 2 < count)
    passes_eight = jnp.logical_and(me >= 4, me + 4 < count)
    for j, valid in ((1, me >= 2), (2, me >= 4), (0, odd)):
        @pl.when(valid)
        def _(j=j):
            feature_copy(j, me - gaps[j]).start()

    for load in loads:
        load.wait()
    wcat[:, :width] = wqk_ref[...]
    wcat[:, width:] = wv_ref[...]
    wcat_t[:width, :] = wqk_ref[...].T
    wcat_t[width:, :] = wv_ref[...].T
    shared = dot(wcat_t[:width, :], x_ref[...], ((1,), (1,))).astype(BF16)
    q_t[...] = (shared.astype(F32) * (1.0 / math.sqrt(head))).astype(BF16)
    dh_t[...] = dot(wout_ref[...], cot_ref[...], ((1,), (1,))).astype(BF16)
    dq_t[...] = jnp.zeros_like(dq_t)
    hid_t[...] = jnp.zeros_like(hid_t)
    acc[...] = jnp.zeros_like(acc)

    def attend(j):
        if j in (0, 3):
            feature_copy(j, me).wait_recv()
        kv_t[...] = dot(wcat_t[...], partner[j], ((1,), (1,))).astype(BF16)

        held = [{} for _ in range(HEADS)]

        def span(h):
            return slice(h * head, (h + 1) * head), slice(width + h * head, width + (h + 1) * head)

        def scored(h):
            first, second = span(h)
            scores = dot(kv_t[first, :], q_t[first, :], ((0,), (0,)))
            d_probs = dot(kv_t[second, :], dh_t[first, :], ((0,), (0,)))
            grown = jnp.exp(scores - jnp.max(scores, axis=0, keepdims=True))
            scale = 1.0 / jnp.sum(grown, axis=0, keepdims=True)
            held[h] = dict(grown=grown, low=grown.astype(BF16), scale=scale, d_probs=d_probs)

        def valued(h):
            first, second = span(h)
            of = held[h]
            of["mixed"] = (dot(kv_t[second, :], of["low"]) * of["scale"]).astype(BF16).astype(F32)
            hid_t[first, :] += of["mixed"]
            scaled = (dh_t[first, :].astype(F32) * of["scale"]).astype(BF16)
            dkv_t[second, :] = dot(scaled, of["low"], ((1,), (1,))).astype(BF16)

        def sloped(h):
            of = held[h]
            rows = jnp.sum(dh_t[span(h)[0], :].astype(F32) * of["mixed"], axis=0, keepdims=True)
            of["d_scores"] = (of["grown"] * (of["d_probs"] - rows)).astype(BF16)

        def returned(h):
            first, second = span(h)
            of = held[h]
            dq_t[first, :] += dot(kv_t[first, :], of["d_scores"]) * of["scale"]
            scaled = (q_t[first, :].astype(F32) * of["scale"]).astype(BF16)
            dkv_t[first, :] = dot(scaled, of["d_scores"], ((1,), (1,))).astype(BF16)

        stages = (scored, valued, sloped, returned)
        for step in range(HEADS + 2 * (len(stages) - 1)):
            for at, stage in enumerate(stages):
                if 0 <= step - 2 * at < HEADS:
                    stage(step - 2 * at)
        kt_send[j] = dot(wcat[...], dkv_t[...]).astype(BF16)
        term_copy(j, me + gaps[j]).start()
        acc[0] += dot(dkv_t[:width, :], partner[j])
        acc[1] += dot(dkv_t[width:, :], partner[j])

    @pl.when(me + 2 < count)
    def _():
        feature_copy(1, me).wait_recv()

    @pl.when(passes_one)
    def _():
        feature_copy(0, me + 1, partner.at[1]).start()

    for j in ORDER:
        if j == ORDER[1]:
            @pl.when(me + 4 < count)
            def _():
                feature_copy(2, me).wait_recv()

            @pl.when(passes_eight)
            def _():
                feature_copy(3, me - 4, partner.at[2]).start()

        @pl.when(me + gaps[j] < count)
        def _(j=j):
            attend(j)

    acc[2] = dot(hid_t[...].astype(BF16), cot_ref[...])
    dq = (dq_t[...] * (1.0 / math.sqrt(head))).astype(BF16)
    acc[0] += dot(dq, x_ref[...])

    chunks = (2, 1, 0)
    last = len(bits) - 1
    paths = {
        c: bits if c != 1 or len(bits) < 4 else [bits[0], bits[2], bits[1]] + bits[3:]
        for c in chunks
    }
    spans = {c: (0, width) for c in chunks}
    copies = []

    def aligned(start, size):
        return pl.ds(pl.multiple_of(start, 16), size)

    def reach(c, s, source, target, sem):
        where = bits.index(paths[c][s])
        copy = pltpu.make_async_remote_copy(
            src_ref=source, dst_ref=target, send_sem=a_send.at[c, sem], recv_sem=a_recv.at[c, sem],
            device_id={"tm": flips[where]}, device_id_type=MESH,
        )
        copy.start()
        copies.append(copy)
        return copy

    def push(c, s):
        start, size = spans[c]
        if s < halvings:
            half = size // 2
            mine = (me // paths[c][s]) % 2
            rows = aligned(start + (1 - mine) * half, half)
            spans[c] = (start + mine * half, half)
            outgoing[c, rows, :] = acc[c, rows, :].astype(BF16)
            return reach(c, s, outgoing.at[c, rows, :], landing[s].at[c], s)
        again[c, s - halvings] = acc[c, aligned(start, size), :].astype(BF16)
        return reach(c, s, again.at[c, s - halvings], landing[s].at[c], s)

    def take(c, s):
        rows = aligned(*spans[c])
        own = acc[c, rows, :]
        if s >= halvings:
            own = again[c, s - halvings].astype(F32)
        acc[c, rows, :] = own + landing[s][c].astype(F32)

    pending = {c: push(c, 0) for c in chunks}
    for s in range(len(bits)):
        for c in chunks:
            pending[c].wait_recv()
            take(c, s)
            if s < last:
                pending[c] = push(c, s + 1)
        if s == 0:
            dq_t[...] = dot(wcat[:, :width], dq)
    for c in chunks:
        rows = aligned(*spans[c])
        result[c, rows, :] = acc[c, rows, :].astype(BF16)

    def spread(c, s):
        start, size = spans[c]
        rows = aligned(start, size)
        spans[c] = (start - ((me // paths[c][s]) % 2) * size, 2 * size)
        sem = len(bits) + s
        return reach(c, s, result.at[c, rows, :], result.at[c, rows, :], sem)

    grad_store = pltpu.make_async_copy(grad_out, grad_hbm, in_sem.at[1])

    def gather_terms():
        for j in ORDER:
            @pl.when(me >= gaps[j])
            def _(j=j):
                term_copy(j, me).wait_recv()
                dq_t[...] += kt_recv[j].astype(F32)
        grad_out[...] = dq_t[...].astype(BF16)
        grad_store.start()

    for s in reversed(range(halvings)):
        if s == halvings - 1:
            pending = {c: spread(c, s) for c in chunks}
            gather_terms()
        for c in chunks:
            pending[c].wait_recv()
            if s > 0:
                pending[c] = spread(c, s - 1)
    if halvings == 0:
        gather_terms()
    store = pltpu.make_async_copy(result, weights_hbm, in_sem.at[0])
    store.start()

    for j, valid in ((0, jnp.logical_or(odd, passes_one)), (1, me >= 2), (2, me >= 4),
                     (3, passes_eight)):
        @pl.when(valid)
        def _(j=j):
            feature_copy(j, me).wait_send()

    for j in ORDER:
        @pl.when(me + gaps[j] < count)
        def _(j=j):
            term_copy(j, me).wait_send()
    for copy in copies:
        copy.wait_send()
    grad_store.wait()
    store.wait()


def finish(norm_factor, grad_ref, sums_ref, *rest):
    outs, held, sems = rest[:4], rest[4:8], rest[8]
    copies = []
    for i in (0, 1, 2, 3):
        if i == 0:
            held[0][...] = grad_ref[...].astype(F32).T.astype(BF16)
        elif i < 3:
            held[i][...] = (sums_ref[i - 1].astype(F32) * norm_factor).T
        else:
            held[i][...] = sums_ref[2].astype(F32) * norm_factor
        copies.append(pltpu.make_async_copy(held[i], outs[i], sems.at[i]))
        copies[-1].start()
    for copy in copies:
        copy.wait()


def shards(count, features, lists, w_qk, w_v, w_out, cotangent):
    tokens, width = features.shape[1:]
    assert lists.shape[2] == lists.shape[3] == 2
    steps = len(bits_of(count))
    halvings = halving_steps(width, count)
    sizes = [width // 2 ** (min(s, halvings - 1) + 1) if s < halvings else width // 2**halvings
             for s in range(steps)]
    vmem = pl.BlockSpec(memory_space=pltpu.VMEM)
    hbm = pl.BlockSpec(memory_space=pltpu.MemorySpace.HBM)
    scratch = [
        pltpu.VMEM((tokens, width), BF16),
        pltpu.VMEM((tokens, width), BF16),
        pltpu.VMEM((width, width), BF16),
        pltpu.VMEM((width, width), BF16),
        pltpu.VMEM((width, width), BF16),
        pltpu.SemaphoreType.DMA((5,)),
        pltpu.VMEM((width, tokens), BF16),
        pltpu.VMEM((width, 2 * width), BF16),
        pltpu.VMEM((2 * width, width), BF16),
        pltpu.VMEM((width, tokens), BF16),
        pltpu.VMEM((width, tokens), BF16),
        pltpu.VMEM((2 * width, tokens), BF16),
        pltpu.VMEM((2 * width, tokens), BF16),
        pltpu.VMEM((width, tokens), F32),
        pltpu.VMEM((width, tokens), F32),
        pltpu.VMEM((NG, tokens, width), BF16),
        pltpu.VMEM((NG, width, tokens), BF16),
        pltpu.VMEM((NG, width, tokens), BF16),
        pltpu.VMEM((3, width, width), F32),
        pltpu.VMEM((3, width, width), BF16),
        pltpu.VMEM((3, width, width), BF16),
        *[pltpu.VMEM((3, size, width), BF16) for size in sizes],
        pltpu.VMEM((3, steps - halvings, width // 2**halvings, width), BF16),
        pltpu.SemaphoreType.DMA((NG,)),
        pltpu.SemaphoreType.DMA((NG,)),
        pltpu.SemaphoreType.DMA((NG,)),
        pltpu.SemaphoreType.DMA((NG,)),
        pltpu.SemaphoreType.DMA((3, 2 * steps)),
        pltpu.SemaphoreType.DMA((3, 2 * steps)),
    ]
    grad_rows, sums = pl.pallas_call(
        functools.partial(kernel, count),
        out_shape=(
            jax.ShapeDtypeStruct((width, tokens), BF16),
            jax.ShapeDtypeStruct((3, width, width), BF16),
        ),
        in_specs=[hbm] * 5,
        out_specs=(hbm, hbm),
        scratch_shapes=scratch,
        compiler_params=pltpu.CompilerParams(collective_id=0, has_side_effects=True),
        name="tracker_backward",
    )(features[0], cotangent[0], w_qk, w_v, w_out)
    norm_factor = 1.0 / math.sqrt(tokens * count)
    shapes = [((tokens, width), BF16)] + [((width, width), F32)] * 3
    grad_rows, *totals = pl.pallas_call(
        functools.partial(finish, norm_factor),
        out_shape=[jax.ShapeDtypeStruct(*shape) for shape in shapes],
        in_specs=[vmem] * 2,
        out_specs=[hbm] * 4,
        scratch_shapes=[pltpu.VMEM(*shape) for shape in shapes] + [pltpu.SemaphoreType.DMA((4,))],
        name="finish",
    )(grad_rows, sums)
    return (grad_rows[None], *totals)


def solution(mesh):
    placed = (
        P(("groups", "tm"), None, None),
        P(None, ("groups", "tm"), None, None),
        P(),
        P(),
        P(),
        P(("groups", "tm"), None, None),
    )
    return jax.shard_map(
        functools.partial(shards, mesh.shape["tm"]),
        mesh=mesh,
        in_specs=placed,
        out_specs=(
            P(("groups", "tm"), None, None),
            P("groups", None),
            P("groups", None),
            P("groups", None),
        ),
        check_vma=False,
    )
```
